512 devices in a mesh: mp: 2 (over x_hi), dp: 32 (over z, core), tensor: 8 (over x_lo, y).
Axes of the slice: x: 4 (x_hi: 2, x_lo: 2; x = x_hi * 2 + x_lo), y: 4, z: 16, core: 2. Of those that a mesh axis runs over, the one named last changes fastest.
Arguments:
- acts: bfloat16 [2, 1024, 8192], P('mp', 'dp', 'tensor'), may hold values from -6 to 6
- gate_w: bfloat16 [2, 8192, 28672], P('mp', 'tensor', 'dp'), may hold values from -0.0625 to 0.0625
- up_w: bfloat16 [2, 8192, 28672], P('mp', 'tensor', 'dp'), may hold values from -0.0625 to 0.0625
- panel_units: int32 [8192], replicated, may hold values from 0 to 28671, as said below
Outputs:
- score: bfloat16 [8192, 28672], P(('mp', 'tensor'), 'dp')
The draws below stay inside these ranges and needn't reach their ends.
Inputs may be any that keep to these rules, and one draw needn't show every extreme that they name: `panel_units`: write an entry's position as ((r * 32) + b) * 16 + k with 0 <= k < 16; the entry lies in [b * 896, (b + 1) * 896), all entries are distinct, and the first and the last unit of every block are among them.
All inputs are finite; a program needn't handle non-finite values.
Results may differ from the reference program's by a relative error of at most 0.03.
Values may be sent and summed in bfloat16 or wider, within the bound.
A program may use at most 64 MiB of HBM per device.

```python
import jax
import jax.numpy as jnp
from jax import lax

D = 8192
FF = 28672
PANEL = 8192
TOKENS = 1024
UNITS_DEV = 896
PER_BLOCK = 256
SELK = 16
N_TENSOR = 8


def draw_panel_units(key, part):
    blocks = FF // UNITS_DEV

    def one_block(index):
        block_key = jax.random.fold_in(key, index)
        order_list = jax.random.permutation(jax.random.fold_in(block_key, 1), UNITS_DEV).astype(jnp.int32)
        local_units = jnp.arange(UNITS_DEV, dtype=jnp.int32)
        at_ends = (local_units == 0) | (local_units == UNITS_DEV - 1)
        ranking = jnp.where(at_ends, -1, order_list)
        chosen = jnp.argsort(ranking, stable=True)[:PER_BLOCK].astype(jnp.int32)
        chosen = jax.random.permutation(jax.random.fold_in(block_key, 2), chosen)
        return chosen + index * UNITS_DEV
    table = jax.vmap(one_block)(jnp.arange(blocks, dtype=jnp.int32))
    table = table.reshape(blocks, PER_BLOCK // SELK, SELK).transpose(1, 0, 2).reshape(-1)
    return table.astype(jnp.int32)


def steps_of(key, shape, pieces, least, top_value):
    def one(dim, blocks):
        heights = jax.random.uniform(jax.random.fold_in(jax.random.fold_in(key, 6), dim), (blocks,), jnp.float32, least / len(pieces), top_value / len(pieces))
        return jnp.repeat(jnp.exp(heights), shape[dim] // blocks).reshape((-1,) + (1,) * (len(shape) - dim - 1))

    loudness = one(*pieces[0])
    for cut in pieces[1:]:
        loudness = loudness * one(*cut)
    return loudness


def centred(key, shape, deviation, limit, split=(), kind=jnp.bfloat16):
    loudness = steps_of(key, shape, split, -0.22, 0.18) if split else 1.0
    entries = jax.random.normal(key, shape, jnp.float32) * deviation * loudness
    return jnp.minimum(jnp.maximum(entries, -limit), limit).astype(kind)


def setup_inputs(seed: int = 0) -> dict:
    seeds = jax.random.split(jax.random.key(seed), 5)
    acts = centred(seeds[0], (2, TOKENS, D), 1.0, 6.0, ((0, 2), (1, 32), (2, 8)))
    gate_w = centred(seeds[1], (2, D, FF), D ** -0.5, 0.0625, ((0, 2), (1, 8), (2, 32)))
    up_w = centred(seeds[2], (2, D, FF), D ** -0.5, 0.0625, ((0, 2), (1, 8), (2, 32)))
    panel_units = draw_panel_units(jax.random.fold_in(seeds[4], 71), 0)
    return dict(acts=acts, gate_w=gate_w, up_w=up_w, panel_units=panel_units)


epsilon = 1e-05

def width_sum(inputs, weight):
    width = D // N_TENSOR

    def add_slice(index, total):
        start = (index * width).astype(jnp.int32)
        rows_slice = lax.dynamic_slice_in_dim(inputs, start, width, 1)
        weight_slice = lax.dynamic_slice_in_dim(weight, start, width, 0)
        partial_sum = jnp.dot(rows_slice, weight_slice, preferred_element_type=jnp.float32)
        rounded = lax.optimization_barrier(partial_sum.astype(jnp.bfloat16))
        return total + rounded.astype(jnp.float32)
    start_total = jnp.zeros((inputs.shape[0], weight.shape[1]), jnp.float32)
    return lax.fori_loop(jnp.int32(0), jnp.int32(N_TENSOR), add_slice, start_total)

def zscores(inputs, weight_gate, weight_up):
    gate = width_sum(inputs, weight_gate)
    upward = width_sum(inputs, weight_up)
    hidden = (jax.nn.silu(gate) * upward).astype(jnp.bfloat16)
    wide_hidden = hidden.astype(jnp.float32)
    unit_mean = lax.optimization_barrier(jnp.mean(wide_hidden, axis=0))
    unit_var = lax.optimization_barrier(jnp.mean(wide_hidden * wide_hidden, axis=0)) - unit_mean * unit_mean
    return ((wide_hidden - unit_mean) * lax.rsqrt(unit_var + epsilon)).astype(jnp.bfloat16)

def reference(acts, gate_w, up_w, panel_units):
    first_z = zscores(acts[0], gate_w[0], up_w[0])
    second_z = zscores(acts[1], gate_w[1], up_w[1])
    panel = jnp.take(first_z, panel_units, axis=1)
    row_size = min(512, PANEL)
    panel_blocks = panel.T.reshape(PANEL // row_size, row_size, TOKENS)
    score_scale = 1.0 / jnp.sqrt(jnp.float32(TOKENS))

    def one_block(rows_block):
        product = jnp.dot(rows_block, second_z, preferred_element_type=jnp.float32)
        return (product * score_scale).astype(jnp.bfloat16)
    result = lax.map(one_block, panel_blocks)
    return result.reshape(PANEL, FF)
```

```python
import functools
import math

import jax
import jax.numpy as jnp
from jax import lax
from jax.experimental import pallas as pl
from jax.experimental.pallas import tpu as pltpu
from jax.sharding import PartitionSpec as P

MESH = pl.DeviceIdType.MESH
F32 = jnp.float32
BF16 = jnp.bfloat16
EPS = 1e-05
TILE = 16
PICK = 16


def wrap(value, n):
    return lax.rem(value + n, n)


def remote(src, dst, send_sem, recv_sem, device):
    return pltpu.make_async_remote_copy(
        src_ref=src,
        dst_ref=dst,
        send_sem=send_sem,
        recv_sem=recv_sem,
        device_id=device,
        device_id_type=MESH,
    )


def silu_times(gate, up):
    return (gate / (1.0 + jnp.exp(-gate)) * up).astype(BF16)


def kernel(
    n_data, n_width, acts_ref, gate_ref, up_ref, table_ref, out_ref,
    xbuf, wg, wu, part_b, got_b, hid_b, sel_w, part_a, got_a, cross_z, panel,
    load_sem, up_s, up_r, dn_s, dn_r, pt_s, pt_r, rs_s, rs_r, ag_s, ag_r,
    xc_s, xc_r, ra_s, ra_r, cz_s, cz_r,
):
    mp = lax.axis_index("mp")
    dp = lax.axis_index("dp")
    t = lax.axis_index("tensor")
    chip = dp // 2
    core = lax.rem(dp, 2)
    n_chip = n_data // 2
    half = n_chip // 2
    rows = acts_ref.shape[1]
    width = acts_ref.shape[2]
    units = gate_ref.shape[2]
    tokens = n_data * rows
    nxt = {"dp": wrap(dp + 2, n_data)}
    prv = {"dp": wrap(dp - 2, n_data)}
    mate_dp = dp + 1 - 2 * core
    mate = {"dp": mate_dp}
    other = {"mp": 1 - mp}
    is_a = mp == 0
    is_b = mp == 1

    def peer_of(d):
        return lax.rem(t + d, n_width)

    loads = [
        pltpu.make_async_copy(acts_ref.at[0], xbuf.at[dp], load_sem.at[0]),
        pltpu.make_async_copy(gate_ref.at[0], wg, load_sem.at[1]),
        pltpu.make_async_copy(up_ref.at[0], wu, load_sem.at[2]),
    ]
    for load in loads:
        load.start()

    barrier = pltpu.get_barrier_semaphore()
    greeted = [nxt, prv, mate, other] + [{"tensor": peer_of(d)} for d in range(1, n_width)]
    for device in greeted:
        pl.semaphore_signal(barrier, inc=1, device_id=device, device_id_type=MESH)
    pl.semaphore_wait(barrier, len(greeted))

    def ring_start(buf, k):
        own = buf.at[dp]
        remote(own, own, up_s.at[k, 1], up_r.at[k, 1], nxt).start()
        remote(own, own, dn_s.at[k, 1], dn_r.at[k, 1], prv).start()
        remote(own, own, pt_s.at[k, 0], pt_r.at[k, 0], mate).start()

    def ring_mate_own(buf, k):
        theirs = buf.at[mate_dp]
        remote(theirs, theirs, pt_s.at[k, 0], pt_r.at[k, 0], mate).wait_recv()

    sides = ((-2, 0, up_s, up_r, nxt, 0), (2, 1, dn_s, dn_r, prv, 1))

    def ring_step(buf, k, s):
        for step, last_core, ss, rs, device, odd in sides:
            @pl.when((s < half) | (core == last_core))
            def _():
                ref = buf.at[wrap(dp + step * s, n_data)]
                remote(ref, ref, ss.at[k, s], rs.at[k, s], device).wait_recv()

                @pl.when((s + 1 < half) | ((s + 1 == half) & (core == last_core)))
                def _():
                    remote(ref, ref, ss.at[k, s + 1], rs.at[k, s + 1], device).start()

                slot = 2 * s + odd
                remote(ref, ref, pt_s.at[k, slot], pt_r.at[k, slot], mate).start()

    def ring_mate(buf, k, s):
        for step, last_core, _ss, _rs, _device, odd in sides:
            @pl.when((s < half) | (core != last_core))
            def _():
                ref = buf.at[wrap(mate_dp + step * s, n_data)]
                slot = 2 * s + odd
                remote(ref, ref, pt_s.at[k, slot], pt_r.at[k, slot], mate).wait_recv()

    def ring_drain(buf, k):
        own = buf.at[dp]
        remote(own, own, pt_s.at[k, 0], pt_r.at[k, 0], mate).wait_send()

        def body(s, carry):
            for _step, last_core, ss, rs, device, odd in sides:
                @pl.when((s < half) | (core == last_core))
                def _():
                    slot = 2 * s + odd
                    remote(own, own, ss.at[k, s], rs.at[k, s], device).wait_send()
                    remote(own, own, pt_s.at[k, slot], pt_r.at[k, slot], mate).wait_send()
            return carry

        lax.fori_loop(1, half + 1, body, 0)

    def chips_of(s):
        return wrap(chip - s, n_chip), lax.rem(chip + lax.rem(s, half), n_chip)

    def tile_of(s, who):
        low, high = chips_of(s)
        quarter = n_width // 2
        return jnp.where(who < quarter, low, high) * quarter + lax.rem(who, quarter)

    def spread(s):
        ref = hid_b.at[tile_of(s, t)]
        for d in range(1, n_width):
            peer = peer_of(d)
            remote(ref, ref, ag_s.at[s - 1, peer], ag_r.at[s - 1, t], {"tensor": peer}).start()

    def b_product(s):
        low, high = chips_of(s)
        x = jnp.concatenate(
            [xbuf[2 * low], xbuf[2 * low + 1], xbuf[2 * high], xbuf[2 * high + 1]], axis=0
        )
        for weight, start in ((wg, 0), (wu, units)):
            y = jnp.dot(x, weight[...], preferred_element_type=F32).astype(BF16)
            part_b[s - 1, :, :, start:start + units] = y.reshape(n_width, TILE, units)
        for d in range(1, n_width):
            peer = peer_of(d)
            remote(
                part_b.at[s - 1, peer], got_b.at[s - 1, t],
                rs_s.at[s - 1, peer], rs_r.at[s - 1, t], {"tensor": peer},
            ).start()

    def b_sum(s):
        total = part_b[s - 1, t].astype(F32)
        for d in range(1, n_width):
            src = peer_of(d)
            ref = got_b.at[s - 1, src]
            remote(ref, ref, rs_s.at[s - 1, src], rs_r.at[s - 1, src], {"tensor": src}).wait_recv()
            total = total + got_b[s - 1, src].astype(F32)
        tile = tile_of(s, t)
        hid_b[tile] = silu_times(total[:, :units], total[:, units:])
        ref = hid_b.at[tile]
        remote(ref, ref, xc_s.at[s - 1], xc_r.at[s - 1], other).start()
        spread(s)

    def a_select():
        blocks_row = n_data // 8
        found = table_ref[pl.ds(dp // 8, 2 * n_width, stride=blocks_row), :]
        found = jnp.broadcast_to(found[:, None, :], (2 * n_width, PICK, 128))
        found = found.reshape(2 * n_width * PICK, 128)
        shape = found.shape
        lane = lax.broadcasted_iota(jnp.int32, shape, 1)
        pick = lax.rem(lax.broadcasted_iota(jnp.int32, shape, 0), PICK)
        wanted = lax.rem(dp, 8) * PICK + pick
        local = jnp.where(lane == wanted, found - dp * units, 0).astype(F32)
        column = jnp.sum(local, axis=1, keepdims=True).astype(jnp.int32)
        unit = lax.broadcasted_iota(jnp.int32, (shape[0], units), 1)
        chosen = jnp.where(unit == column, 1.0, 0.0).astype(BF16)
        for i, weight in enumerate((wg, wu)):
            sel_w[i] = lax.dot_general(
                chosen, weight[...], (((1,), (1,)), ((), ())), preferred_element_type=F32
            ).astype(BF16)

    def a_product():
        span = 4 * 2 * rows

        def body(i, carry):
            blocks = span // rows
            x = xbuf[pl.ds(i * blocks, blocks)].reshape(span, width)
            columns = pl.ds(pl.multiple_of(i * span, span), span)
            for kind in range(2):
                y = lax.dot_general(
                    sel_w[kind], x, (((1,), (1,)), ((), ())), preferred_element_type=F32
                ).astype(BF16)
                for r in range(2 * n_width):
                    part_a[r // n_width, r % n_width, kind, :, columns] = y[r * PICK:(r + 1) * PICK]
            return carry

        lax.fori_loop(0, tokens // span, body, 0)
        for d in range(1, n_width):
            peer = peer_of(d)
            remote(
                part_a.at[:, peer], got_a.at[t], ra_s.at[peer], ra_r.at[t], {"tensor": peer}
            ).start()

    def a_sum():
        for d in range(1, n_width):
            src = peer_of(d)
            ref = got_a.at[src]
            remote(ref, ref, ra_s.at[src], ra_r.at[src], {"tensor": src}).wait_recv()
        for group in (1, 0):
            gate = part_a[group, t, 0].astype(F32)
            up = part_a[group, t, 1].astype(F32)
            for d in range(1, n_width):
                gate = gate + got_a[peer_of(d), group, 0].astype(F32)
                up = up + got_a[peer_of(d), group, 1].astype(F32)
            wide = silu_times(gate, up).astype(F32)
            mean = jnp.sum(wide, axis=1, keepdims=True) / tokens
            var = jnp.sum(wide * wide, axis=1, keepdims=True) / tokens - mean * mean
            z = ((wide - mean) * lax.rsqrt(var + EPS)).astype(BF16)
            if group == 1:
                cross_z[...] = z
                remote(cross_z, panel.at[dp], cz_s.at[0], cz_r.at[0], other).start()
            else:
                panel[dp] = z

    loads[0].wait()
    ring_start(xbuf, 0)
    loads[1].wait()
    loads[2].wait()

    @pl.when(is_a)
    def _():
        a_select()

    ring_mate_own(xbuf, 0)

    def gather_step(s, carry):
        ring_step(xbuf, 0, s)
        ring_mate(xbuf, 0, s)

        @pl.when(is_b)
        def _():
            b_product(s)

        return carry

    lax.fori_loop(1, half + 1, gather_step, 0)

    @pl.when(is_a)
    def _():
        a_product()
        a_sum()
        ring_start(panel, 1)

        def step(s, carry):
            ring_step(panel, 1, s)
            ring_mate(panel, 1, s)
            ref = hid_b.at[tile_of(s, t)]
            remote(ref, ref, xc_s.at[s - 1], xc_r.at[s - 1], other).wait_recv()
            spread(s)
            return carry

        lax.fori_loop(1, half + 1, step, 0)

    @pl.when(is_b)
    def _():
        def early(s, carry):
            b_sum(s)
            return carry

        lax.fori_loop(1, half // 2 + 1, early, 0)
        own = panel.at[dp]
        remote(own, own, cz_s.at[0], cz_r.at[0], other).wait_recv()
        ring_start(panel, 1)

        def late(s, carry):
            b_sum(half // 2 + s)
            for j in (2 * s - 1, 2 * s):
                ring_step(panel, 1, j)
                ring_mate(panel, 1, j)
            return carry

        lax.fori_loop(1, half // 2 + 1, late, 0)

    ring_mate_own(panel, 1)

    def arrive(s, carry):
        for d in range(1, n_width):
            src = peer_of(d)
            ref = hid_b.at[tile_of(s, src)]
            remote(ref, ref, ag_s.at[s - 1, src], ag_r.at[s - 1, src], {"tensor": src}).wait_recv()
        return carry

    lax.fori_loop(1, half + 1, arrive, 0)

    left = panel[...].reshape(n_data * PICK, tokens)
    scale = 1.0 / math.sqrt(tokens)
    start = 0
    while start < units:
        size = min(256, units - start)
        wide = hid_b[:, :, start:start + size].reshape(tokens, size).astype(F32)
        mean = jnp.sum(wide, axis=0, keepdims=True) / tokens
        var = jnp.sum(wide * wide, axis=0, keepdims=True) / tokens - mean * mean
        z = ((wide - mean) * lax.rsqrt(var + EPS)).astype(BF16)
        score = jnp.dot(left, z, preferred_element_type=F32) * scale
        out_ref[:, start:start + size] = score.astype(BF16)
        start += size

    ring_drain(xbuf, 0)
    ring_drain(panel, 1)

    def sent(s, carry):
        for d in range(1, n_width):
            peer = peer_of(d)
            ref = hid_b.at[tile_of(s, t)]
            remote(ref, ref, ag_s.at[s - 1, peer], ag_r.at[s - 1, t], {"tensor": peer}).wait_send()

            @pl.when(is_b)
            def _():
                src = part_b.at[s - 1, peer]
                remote(src, src, rs_s.at[s - 1, peer], rs_r.at[s - 1, t], {"tensor": peer}).wait_send()

        @pl.when(is_b)
        def _():
            mine = hid_b.at[tile_of(s, t)]
            remote(mine, mine, xc_s.at[s - 1], xc_r.at[s - 1], other).wait_send()

        return carry

    lax.fori_loop(1, half + 1, sent, 0)

    @pl.when(is_a)
    def _():
        remote(cross_z, panel.at[dp], cz_s.at[0], cz_r.at[0], other).wait_send()
        for d in range(1, n_width):
            peer = peer_of(d)
            remote(
                part_a.at[:, peer], got_a.at[t], ra_s.at[peer], ra_r.at[t], {"tensor": peer}
            ).wait_send()


def body(n_data, n_width, acts, gate_w, up_w, panel_units):
    _, rows, width = acts.shape
    units = gate_w.shape[2]
    tokens = n_data * rows
    steps = n_data // 4
    any_space = pl.BlockSpec(memory_space=pl.ANY)
    vmem = pl.BlockSpec(memory_space=pltpu.VMEM)
    dma = pltpu.SemaphoreType.DMA
    return pl.pallas_call(
        functools.partial(kernel, n_data, n_width),
        out_shape=jax.ShapeDtypeStruct((n_data * PICK, units), BF16),
        in_specs=[any_space, any_space, any_space, vmem],
        out_specs=vmem,
        scratch_shapes=[
            pltpu.VMEM((n_data, rows, width), BF16),
            pltpu.VMEM((width, units), BF16),
            pltpu.VMEM((width, units), BF16),
            pltpu.VMEM((steps, n_width, TILE, 2 * units), BF16),
            pltpu.VMEM((steps, n_width, TILE, 2 * units), BF16),
            pltpu.VMEM((tokens // TILE, TILE, units), BF16),
            pltpu.VMEM((2, 2 * n_width * PICK, width), BF16),
            pltpu.VMEM((2, n_width, 2, PICK, tokens), BF16),
            pltpu.VMEM((n_width, 2, 2, PICK, tokens), BF16),
            pltpu.VMEM((PICK, tokens), BF16),
            pltpu.VMEM((n_data, PICK, tokens), BF16),
            dma((3,)),
            dma((2, steps + 1)),
            dma((2, steps + 1)),
            dma((2, steps + 1)),
            dma((2, steps + 1)),
            dma((2, 2 * steps + 2)),
            dma((2, 2 * steps + 2)),
            dma((steps, n_width)),
            dma((steps, n_width)),
            dma((steps, n_width)),
            dma((steps, n_width)),
            dma((steps,)),
            dma((steps,)),
            dma((n_width,)),
            dma((n_width,)),
            dma((1,)),
            dma((1,)),
        ],
        compiler_params=pltpu.CompilerParams(
            collective_id=0, has_side_effects=True, vmem_limit_bytes=60 * 1024 * 1024
        ),
    )(acts, gate_w, up_w, panel_units.reshape(-1, 128))


def solution(mesh):
    in_specs = (P("mp", "dp", "tensor"), P("mp", "tensor", "dp"), P("mp", "tensor", "dp"), P())
    out_specs = P(("mp", "tensor"), "dp")
    step = functools.partial(body, mesh.shape["dp"], mesh.shape["tensor"])
    return jax.shard_map(step, mesh=mesh, in_specs=in_specs, out_specs=out_specs, check_vma=False)
```

```python
import functools
import math

import jax
import jax.numpy as jnp
from jax import lax
from jax.experimental import pallas as pl
from jax.experimental.pallas import tpu as pltpu
from jax.sharding import PartitionSpec as P

MESH = pl.DeviceIdType.MESH
F32 = jnp.float32
BF16 = jnp.bfloat16
EPS = 1e-05
TILE = 16
PICK = 16


def wrap(value, n):
    return lax.rem(value + n, n)


def remote(src, dst, send_sem, recv_sem, device):
    return pltpu.make_async_remote_copy(
        src_ref=src,
        dst_ref=dst,
        send_sem=send_sem,
        recv_sem=recv_sem,
        device_id=device,
        device_id_type=MESH,
    )


def silu_times(gate, up):
    return (gate / (1.0 + jnp.exp(-gate)) * up).astype(BF16)


def kernel(
    n_data, n_width, acts_ref, gate_ref, up_ref, table_ref, out_ref,
    xbuf, wg, wu, part_b, got_x, sum_b, got_y, hid_b, sel_w, part_a, got_a, cross_z, panel,
    load_sem, up_s, up_r, dn_s, dn_r, pt_s, pt_r, px_s, px_r, rx_s, rx_r, ry_s, ry_r,
    gx_s, gx_r, g1_s, g1_r, g2_s, g2_r, xc_s, xc_r, ra_s, ra_r, cz_s, cz_r,
):
    mp = lax.axis_index("mp")
    dp = lax.axis_index("dp")
    t = lax.axis_index("tensor")
    chip = dp // 2
    core = lax.rem(dp, 2)
    n_chip = n_data // 2
    half = n_chip // 2
    reach = half // 2
    n_pair = n_chip // 2
    n_y = n_width // 2
    x = t // n_y
    y = lax.rem(t, n_y)
    rows = acts_ref.shape[1]
    width = acts_ref.shape[2]
    units = gate_ref.shape[2]
    tokens = n_data * rows
    nxt = {"dp": wrap(dp + 2, n_data)}
    prv = {"dp": wrap(dp - 2, n_data)}
    mate_dp = dp + 1 - 2 * core
    mate = {"dp": mate_dp}
    across_t = lax.rem(t + n_y, n_width)
    across = {"tensor": across_t}
    other = {"mp": 1 - mp, "tensor": across_t}
    is_a = mp == 0
    is_b = mp == 1

    helped = [s for s in (1, 3) if s <= half]

    def is_helped(s):
        return functools.reduce(jnp.logical_or, [s == h for h in helped])

    def is_owner(s):
        return jnp.logical_not(jnp.logical_xor(is_a, is_helped(s)))

    def mine(s):
        return jnp.where(is_owner(s), t, across_t)

    def theirs(s):
        return jnp.where(is_owner(s), across_t, t)

    def peer_of(d):
        return lax.rem(t + d, n_width)

    def y_of(d):
        return lax.rem(y + d, n_y)

    def at_y(row):
        return {"tensor": x * n_y + row}

    loads = [
        pltpu.make_async_copy(acts_ref.at[0], xbuf.at[dp], load_sem.at[0]),
        pltpu.make_async_copy(gate_ref.at[0], wg, load_sem.at[1]),
        pltpu.make_async_copy(up_ref.at[0], wu, load_sem.at[2]),
    ]
    for load in loads:
        load.start()

    barrier = pltpu.get_barrier_semaphore()
    greeted = [mate, other] + [{"tensor": peer_of(d)} for d in range(1, n_width)]
    for d in range(1, reach + 1):
        greeted += [{"dp": wrap(dp + 2 * d, n_data)}, {"dp": wrap(dp - 2 * d, n_data)}]
    for device in greeted:
        pl.semaphore_signal(barrier, inc=1, device_id=device, device_id_type=MESH)
    pl.semaphore_wait(barrier, len(greeted))

    sides = ((-2, 0, up_s, up_r, nxt, 0), (2, 1, dn_s, dn_r, prv, 1))
    acts_ring = (xbuf, tuple((k, pl.ds(k * TILE, TILE)) for k in range(rows // TILE)))
    spread = rows // TILE

    def ring_start(ring):
        buf, pieces = ring
        for k, part in pieces:
            own = buf.at[dp, part]
            for _step, _last, ss, rs, device, _odd in sides:
                remote(own, own, ss.at[k, 1], rs.at[k, 1], device).start()
            remote(own, own, pt_s.at[k, 0], pt_r.at[k, 0], mate).start()

    def ring_mate_own(ring):
        buf, pieces = ring
        for k, part in pieces:
            theirs = buf.at[mate_dp, part]
            remote(theirs, theirs, pt_s.at[k, 0], pt_r.at[k, 0], mate).wait_recv()

    def ring_step(ring, s):
        buf, pieces = ring
        for k, part in pieces:
            for step, last_core, ss, rs, device, odd in sides:
                @pl.when((s < half) | (core == last_core))
                def _():
                    ref = buf.at[wrap(dp + step * s, n_data), part]
                    remote(ref, ref, ss.at[k, s], rs.at[k, s], device).wait_recv()

                    @pl.when((s + 1 < half) | ((s + 1 == half) & (core == last_core)))
                    def _():
                        remote(ref, ref, ss.at[k, s + 1], rs.at[k, s + 1], device).start()

                    slot = 2 * s + odd
                    remote(ref, ref, pt_s.at[k, slot], pt_r.at[k, slot], mate).start()

    def ring_mate(ring, s):
        buf, pieces = ring
        for k, part in pieces:
            for step, last_core, _ss, _rs, _device, odd in sides:
                @pl.when((s < half) | (core != last_core))
                def _():
                    ref = buf.at[wrap(mate_dp + step * s, n_data), part]
                    slot = 2 * s + odd
                    remote(ref, ref, pt_s.at[k, slot], pt_r.at[k, slot], mate).wait_recv()

    def ring_drain(buf, pieces):
        for k, part in pieces:
            own = buf.at[dp, part]
            remote(own, own, pt_s.at[k, 0], pt_r.at[k, 0], mate).wait_send()

            def body(s, carry):
                for _step, last_core, ss, rs, device, odd in sides:
                    @pl.when((s < half) | (core == last_core))
                    def _():
                        slot = 2 * s + odd
                        remote(own, own, ss.at[k, s], rs.at[k, s], device).wait_send()
                        remote(own, own, pt_s.at[k, slot], pt_r.at[k, slot], mate).wait_send()
                return carry

            lax.fori_loop(1, half + 1, body, 0)

    def panel_start():
        own = panel.at[dp]
        for d in range(reach, 0, -1):
            for step, _last, ss, rs, _device, _odd in sides:
                target = {"dp": wrap(dp - step * d, n_data)}
                remote(own, own, ss.at[spread, d], rs.at[spread, d], target).start()
        remote(own, own, pt_s.at[spread, 0], pt_r.at[spread, 0], mate).start()

    def panel_take(d, side):
        step, _last, ss, rs, device, odd = side
        ref = panel.at[wrap(dp + step * d, n_data)]
        remote(ref, ref, ss.at[spread, d], rs.at[spread, d], device).wait_recv()
        return ref, remote(
            ref, ref, pt_s.at[spread, 2 * d + odd], pt_r.at[spread, 2 * d + odd], mate
        )

    def panel_take_own():
        own = panel.at[dp]
        remote(own, own, cz_s.at[0], cz_r.at[0], other).wait_recv()

    def panel_forward():
        for side in sides:
            step, last_core, ss, rs, _device, _odd = side
            ref, to_mate = panel_take(reach, side)

            def pass_to(d):
                target = {"dp": wrap(dp - step * d, n_data)}
                return remote(ref, ref, ss.at[spread, reach + d], rs.at[spread, reach + d], target)

            @pl.when(core == last_core)
            def _():
                pass_to(reach).start()

            for d in range(reach - 1, 0, -1):
                pass_to(d).start()
            to_mate.start()

    def panel_collect():
        for d in range(1, half + 1):
            if d == reach:
                continue
            for side in sides:
                if d < half:
                    panel_take(d, side)[1].start()
                else:
                    @pl.when(core == side[1])
                    def _():
                        panel_take(d, side)[1].start()

    def panel_mate():
        theirs = panel.at[mate_dp]
        remote(theirs, theirs, pt_s.at[spread, 0], pt_r.at[spread, 0], mate).wait_recv()

        def body(d, carry):
            for step, last_core, _ss, _rs, _device, odd in sides:
                @pl.when((d < half) | (core != last_core))
                def _():
                    ref = panel.at[wrap(mate_dp + step * d, n_data)]
                    slot = 2 * d + odd
                    remote(
                        ref, ref, pt_s.at[spread, slot], pt_r.at[spread, slot], mate
                    ).wait_recv()
            return carry

        lax.fori_loop(1, half + 1, body, 0)

    def tile_of(s, who):
        low, high = wrap(chip - s, n_chip), lax.rem(chip + lax.rem(s, half), n_chip)
        return jnp.where(who < n_y, low, high) * n_y + lax.rem(who, n_y)

    def own_copies(s):
        ref = hid_b.at[tile_of(s, mine(s))]
        copies = [remote(ref, ref, gx_s.at[s - 1], gx_r.at[s - 1], across)]
        for d in range(1, n_y):
            row = y_of(d)
            copies.append(remote(ref, ref, g1_s.at[s - 1, row], g1_r.at[s - 1, y], at_y(row)))
        return copies

    def passed_copies(s):
        ref = hid_b.at[tile_of(s, theirs(s))]
        return [
            remote(ref, ref, g2_s.at[s - 1, y_of(d)], g2_r.at[s - 1, y], at_y(y_of(d)))
            for d in range(1, n_y)
        ]

    def direct_copies(s):
        ref = hid_b.at[tile_of(s, mine(s))]
        return [
            remote(
                ref, ref, g2_s.at[s - 1, y_of(d)], g2_r.at[s - 1, y],
                {"tensor": (1 - x) * n_y + y_of(d)},
            )
            for d in range(1, n_y)
        ]

    def cross_copy(s, who):
        ref = hid_b.at[tile_of(s, who)]
        return remote(ref, ref, xc_s.at[s - 1], xc_r.at[s - 1], other)

    def pass_on(s):
        ref = hid_b.at[tile_of(s, theirs(s))]
        remote(ref, ref, gx_s.at[s - 1], gx_r.at[s - 1], across).wait_recv()
        for copy in passed_copies(s):
            copy.start()

    def x_copy(s):
        return remote(
            part_b.at[s - 1, pl.ds((1 - x) * n_y, n_y)], got_x.at[s - 1],
            rx_s.at[s - 1], rx_r.at[s - 1], across,
        )

    def raw_copy(s):
        ref = part_b.at[s - 1]
        return remote(ref, ref, px_s.at[s - 1], px_r.at[s - 1], other)

    def raw(s):
        raw_copy(s).wait_recv()
        x_copy(s).start()

    def y_copy(s, row):
        return remote(
            sum_b.at[s - 1, row], got_y.at[s - 1, y], ry_s.at[s - 1, row], ry_r.at[s - 1, y], at_y(row)
        )

    def b_product(s):
        low, high = wrap(chip - s, n_chip), lax.rem(chip + lax.rem(s, half), n_chip)
        left = jnp.concatenate(
            [xbuf[2 * low], xbuf[2 * low + 1], xbuf[2 * high], xbuf[2 * high + 1]], axis=0
        )
        for weight, start in ((wg, 0), (wu, units)):
            part = jnp.dot(left, weight[...], preferred_element_type=F32).astype(BF16)
            part_b[s - 1, :, :, start:start + units] = part.reshape(n_width, TILE, units)
        @pl.when(is_helped(s))
        def _():
            raw_copy(s).start()

        @pl.when(jnp.logical_not(is_helped(s)))
        def _():
            x_copy(s).start()

    def b_pair(s):
        x_copy(s).wait_recv()
        for d in range(1, n_y):
            row = y_of(d)
            pair = part_b[s - 1, x * n_y + row].astype(F32) + got_x[s - 1, row].astype(F32)
            sum_b[s - 1, row] = pair.astype(BF16)
            y_copy(s, row).start()

    def b_total(s):
        total = part_b[s - 1, t].astype(F32) + got_x[s - 1, y].astype(F32)
        for d in range(1, n_y):
            row = y_of(d)
            ref = got_y.at[s - 1, row]
            remote(ref, ref, ry_s.at[s - 1, row], ry_r.at[s - 1, row], at_y(row)).wait_recv()
            total = total + got_y[s - 1, row].astype(F32)
        hid_b[tile_of(s, t)] = silu_times(total[:, :units], total[:, units:])
        cross_copy(s, t).start()
        share(s)

    def share(s):
        for copy in own_copies(s):
            copy.start()

        @pl.when(is_a | (s == half))
        def _():
            for copy in direct_copies(s):
                copy.start()

    def take(s):
        cross_copy(s, mine(s)).wait_recv()
        share(s)

    def a_select():
        found = table_ref[pl.ds(dp // 8, 2 * n_width, stride=n_data // 8), :]
        found = jnp.broadcast_to(found[:, None, :], (2 * n_width, PICK, 128))
        found = found.reshape(2 * n_width * PICK, 128)
        shape = found.shape
        lane = lax.broadcasted_iota(jnp.int32, shape, 1)
        pick = lax.rem(lax.broadcasted_iota(jnp.int32, shape, 0), PICK)
        wanted = lax.rem(dp, 8) * PICK + pick
        local = jnp.where(lane == wanted, found - dp * units, 0).astype(F32)
        column = jnp.sum(local, axis=1, keepdims=True).astype(jnp.int32)
        unit = lax.broadcasted_iota(jnp.int32, (shape[0], units), 1)
        chosen = jnp.where(unit == column, 1.0, 0.0).astype(BF16)
        for i, weight in enumerate((wg, wu)):
            sel_w[i] = lax.dot_general(
                chosen, weight[...], (((1,), (1,)), ((), ())), preferred_element_type=F32
            ).astype(BF16)

    def a_copy(pair, peer):
        return remote(
            part_a.at[pair, :, peer], got_a.at[t, pair], ra_s.at[pair, peer], ra_r.at[pair, t],
            {"tensor": peer},
        )

    def a_product(pair):
        blocks = 128 // rows
        right = xbuf[pl.ds(pair * blocks, blocks)].reshape(128, width)
        for kind in range(2):
            part = lax.dot_general(
                sel_w[kind], right, (((1,), (1,)), ((), ())), preferred_element_type=F32
            ).astype(BF16)
            for r in range(2 * n_width):
                group = r // n_width
                who = (r + group * n_y) % n_width
                part_a[pair, group, who, kind] = part[r * PICK:(r + 1) * PICK]
        for d in range(1, n_width):
            a_copy(pair, peer_of(d)).start()

    def a_chunk(s):
        here = chip // 2
        k = s // 2
        odd = lax.rem(s, 2) == 1

        @pl.when(odd)
        def _():
            a_product(lax.rem(here + k, n_pair))

        @pl.when(odd & (s > 1))
        def _():
            a_product(wrap(here - k, n_pair))

        @pl.when(s == half)
        def _():
            a_product(lax.rem(here + n_pair // 2, n_pair))

    def a_sum():
        def body(pair, carry):
            for d in range(1, n_width):
                src = peer_of(d)
                ref = got_a.at[src, pair]
                remote(
                    ref, ref, ra_s.at[pair, src], ra_r.at[pair, src], {"tensor": src}
                ).wait_recv()
            return carry

        lax.fori_loop(0, n_pair, body, 0)
        for group in (1, 0):
            pieces = []
            for pair in range(n_pair):
                gate = part_a[pair, group, t, 0].astype(F32)
                up = part_a[pair, group, t, 1].astype(F32)
                for d in range(1, n_width):
                    gate = gate + got_a[peer_of(d), pair, group, 0].astype(F32)
                    up = up + got_a[peer_of(d), pair, group, 1].astype(F32)
                pieces.append(silu_times(gate, up).astype(F32))
            wide = jnp.concatenate(pieces, axis=1)
            mean = jnp.sum(wide, axis=1, keepdims=True) / tokens
            var = jnp.sum(wide * wide, axis=1, keepdims=True) / tokens - mean * mean
            z = ((wide - mean) * lax.rsqrt(var + EPS)).astype(BF16)
            if group == 1:
                cross_z[...] = z
                remote(cross_z, panel.at[dp], cz_s.at[0], cz_r.at[0], other).start()
            else:
                panel[dp] = z

    loads[0].wait()
    ring_start(acts_ring)
    loads[1].wait()
    loads[2].wait()

    @pl.when(is_a)
    def _():
        a_select()

    ring_mate_own(acts_ring)

    def use(s):
        ring_mate(acts_ring, s)

        @pl.when(is_b)
        def _():
            b_product(s)

        @pl.when(is_a)
        def _():
            a_chunk(s)

    owned = [s for s in range(1, half + 1) if s not in helped]
    if half == 8:
        a_early = [(6, raw, 1), (8, take, 2)]
        b_early = [(6, b_pair, 2), (7, b_total, 2), (8, b_pair, 4)]
        a_late = [
            (b_pair, 1), (raw, 3), (b_total, 1), (a_sum,), (panel_start,), (b_pair, 3), (take, 4),
            (b_total, 3), (take, 5), (panel_forward,), (take, 6), (take, 7), (panel_collect,),
            (take, 8),
        ]
        b_late = [
            (b_total, 4), (b_pair, 5), (b_pair, 6), (b_total, 5), (take, 1), (b_pair, 7),
            (b_total, 6), (panel_take_own,), (panel_start,), (b_total, 7), (b_pair, 8), (take, 3),
            (panel_forward,), (b_total, 8), *[(pass_on, s) for s in (2, 4, 5, 1, 6, 7, 3)],
            (panel_collect,),
        ]
    else:
        a_early, b_early = [], []
        a_late = [
            *[(act, s) for s in helped for act in (raw, b_pair, b_total)], (a_sum,), (panel_start,),
            *[(take, s) for s in owned], (panel_forward,), (panel_collect,),
        ]
        b_late = [
            *[(act, s) for s in owned for act in (b_pair, b_total)], (panel_take_own,),
            (panel_start,), *[(take, s) for s in helped], (panel_forward,),
            *[(pass_on, s) for s in range(1, half)], (panel_collect,),
        ]

    def gather_step(s, carry):
        ring_step(acts_ring, s)

        @pl.when(s > 1)
        def _():
            use(s - 1)

        for model, when in ((is_a, a_early), (is_b, b_early)):
            for step, act, chunk in when:
                @pl.when(model & (s == step))
                def _():
                    act(chunk)

        return carry

    lax.fori_loop(1, half + 1, gather_step, 0)
    use(half)

    for model, acts in ((is_a, a_late), (is_b, b_late)):
        @pl.when(model)
        def _():
            for act, *chunk in acts:
                act(*chunk)

    def last(s, carry):
        @pl.when(is_a | (s == half))
        def _():
            ref = hid_b.at[tile_of(s, theirs(s))]
            remote(ref, ref, gx_s.at[s - 1], gx_r.at[s - 1], across).wait_recv()

        return carry

    ring_drain(*acts_ring)
    ring_drain(panel, ((spread, pl.ds(0, PICK)),))
    lax.fori_loop(1, half + 1, last, 0)
    panel_mate()

    def arrive(s, carry):
        for d in range(1, n_y):
            row = y_of(d)
            first = hid_b.at[tile_of(s, mine(s) // n_y * n_y + row)]
            remote(first, first, g1_s.at[s - 1, row], g1_r.at[s - 1, row], at_y(row)).wait_recv()
            second = hid_b.at[tile_of(s, theirs(s) // n_y * n_y + row)]
            remote(second, second, g2_s.at[s - 1, row], g2_r.at[s - 1, row], at_y(row)).wait_recv()
        return carry

    lax.fori_loop(1, half + 1, arrive, 0)

    left = panel[...].reshape(n_data * PICK, tokens)
    scale = 1.0 / math.sqrt(tokens)
    start = 0
    while start < units:
        size = min(256, units - start)
        wide = hid_b[:, :, start:start + size].reshape(tokens, size).astype(F32)
        mean = jnp.sum(wide, axis=0, keepdims=True) / tokens
        var = jnp.sum(wide * wide, axis=0, keepdims=True) / tokens - mean * mean
        z = ((wide - mean) * lax.rsqrt(var + EPS)).astype(BF16)
        score = jnp.dot(left, z, preferred_element_type=F32) * scale
        out_ref[:, start:start + size] = score.astype(BF16)
        start += size

    def sent(s, carry):
        for copy in own_copies(s) + passed_copies(s):
            copy.wait_send()

        @pl.when(is_owner(s))
        def _():
            cross_copy(s, t).wait_send()
            x_copy(s).wait_send()
            for d in range(1, n_y):
                y_copy(s, y_of(d)).wait_send()

        @pl.when(is_b & is_helped(s))
        def _():
            raw_copy(s).wait_send()

        return carry

    lax.fori_loop(1, half + 1, sent, 0)

    @pl.when(is_a)
    def _():
        remote(cross_z, panel.at[dp], cz_s.at[0], cz_r.at[0], other).wait_send()

        def body(pair, carry):
            for d in range(1, n_width):
                a_copy(pair, peer_of(d)).wait_send()
            return carry

        lax.fori_loop(0, n_pair, body, 0)


def body(n_data, n_width, acts, gate_w, up_w, panel_units):
    _, rows, width = acts.shape
    units = gate_w.shape[2]
    tokens = n_data * rows
    steps = n_data // 4
    pairs = n_data // 4
    n_y = n_width // 2
    rings = rows // TILE + 1
    hbm = pl.BlockSpec(memory_space=pltpu.HBM)
    vmem = pl.BlockSpec(memory_space=pltpu.VMEM)
    dma = pltpu.SemaphoreType.DMA
    both = lambda *shape: [dma(shape), dma(shape)]
    return pl.pallas_call(
        functools.partial(kernel, n_data, n_width),
        out_shape=jax.ShapeDtypeStruct((n_data * PICK, units), BF16),
        in_specs=[hbm, hbm, hbm, vmem],
        out_specs=vmem,
        scratch_shapes=[
            pltpu.VMEM((n_data, rows, width), BF16),
            pltpu.VMEM((width, units), BF16),
            pltpu.VMEM((width, units), BF16),
            pltpu.VMEM((steps, n_width, TILE, 2 * units), BF16),
            pltpu.VMEM((steps, n_y, TILE, 2 * units), BF16),
            pltpu.VMEM((steps, n_y, TILE, 2 * units), BF16),
            pltpu.VMEM((steps, n_y, TILE, 2 * units), BF16),
            pltpu.VMEM((tokens // TILE, TILE, units), BF16),
            pltpu.VMEM((2, 2 * n_width * PICK, width), BF16),
            pltpu.VMEM((pairs, 2, n_width, 2, PICK, 128), BF16),
            pltpu.VMEM((n_width, pairs, 2, 2, PICK, 128), BF16),
            pltpu.VMEM((PICK, tokens), BF16),
            pltpu.VMEM((n_data, PICK, tokens), BF16),
            dma((3,)),
            *both(rings, steps + 1),
            *both(rings, steps + 1),
            *both(rings, 2 * steps + 2),
            *both(steps),
            *both(steps),
            *both(steps, n_y),
            *both(steps),
            *both(steps, n_y),
            *both(steps, n_y),
            *both(steps),
            *both(pairs, n_width),
            *both(1),
        ],
        compiler_params=pltpu.CompilerParams(
            collective_id=0, has_side_effects=True, vmem_limit_bytes=62914560
        ),
    )(acts, gate_w, up_w, panel_units.reshape(-1, 128))


def solution(mesh):
    in_specs = (P("mp", "dp", "tensor"), P("mp", "tensor", "dp"), P("mp", "tensor", "dp"), P())
    out_specs = P(("mp", "tensor"), "dp")
    step = functools.partial(body, mesh.shape["dp"], mesh.shape["tensor"])
    return jax.shard_map(step, mesh=mesh, in_specs=in_specs, out_specs=out_specs, check_vma=False)
```

```python
import functools
import math

import jax
import jax.numpy as jnp
from jax import lax
from jax.experimental import pallas as pl
from jax.experimental.pallas import tpu as pltpu
from jax.sharding import PartitionSpec as P

MESH = pl.DeviceIdType.MESH
F32 = jnp.float32
BF16 = jnp.bfloat16
EPS = 1e-05
TILE = 16
PICK = 16


def wrap(value, n):
    return lax.rem(value + n, n)


def remote(src, dst, send_sem, recv_sem, device):
    return pltpu.make_async_remote_copy(
        src_ref=src,
        dst_ref=dst,
        send_sem=send_sem,
        recv_sem=recv_sem,
        device_id=device,
        device_id_type=MESH,
    )


def silu_times(gate, up):
    return (gate / (1.0 + jnp.exp(-gate)) * up).astype(BF16)


def kernel(
    n_data, n_width, acts_ref, gate_ref, up_ref, table_ref, out_ref,
    xbuf, wg, wu, part_b, got_x, sum_b, got_y, got_d, hid_b, sel_w, part_a, got_a, cross_z, panel,
    load_sem, up_s, up_r, dn_s, dn_r, pt_s, pt_r, px_s, px_r, bk_s, bk_r, rd_s, rd_r, rx_s, rx_r, ry_s, ry_r,
    gx_s, gx_r, g_s, g_r, xc_s, xc_r, ra_s, ra_r, cz_s, cz_r,
):
    mp = lax.axis_index("mp")
    dp = lax.axis_index("dp")
    t = lax.axis_index("tensor")
    chip = dp // 2
    core = lax.rem(dp, 2)
    n_chip = n_data // 2
    half = n_chip // 2
    reach = half // 2
    n_pair = n_chip // 2
    n_y = n_width // 2
    x = t // n_y
    y = lax.rem(t, n_y)
    rows = acts_ref.shape[1]
    width = acts_ref.shape[2]
    units = gate_ref.shape[2]
    tokens = n_data * rows
    mate_dp = dp + 1 - 2 * core
    mate = {"dp": mate_dp}
    across_t = lax.rem(t + n_y, n_width)
    across = {"tensor": across_t}
    other = {"mp": 1 - mp, "tensor": across_t}
    is_a = mp == 0
    is_b = mp == 1

    helped = [s for s in (1, 3) if s <= half]

    def is_helped(s):
        return functools.reduce(jnp.logical_or, [s == h for h in helped])

    relayed = (1, 2, 4, 5) if half == 8 else ()
    first_late = 6 if half == 8 else half + 1

    def is_direct(s):
        passed = functools.reduce(jnp.logical_or, [s == r for r in relayed], s < 0)
        return jnp.where(is_a, jnp.logical_not(passed), s == half)

    full = [s for s in (2, 4) if s <= half]

    def is_full(s):
        return functools.reduce(jnp.logical_or, [s == f for f in full])

    returned = [s for s in ((1, 2, 4) if half == 8 else (2,)) if s <= half]

    def is_returned(s):
        return functools.reduce(jnp.logical_or, [s == r for r in returned])

    def is_owner(s):
        return jnp.logical_not(jnp.logical_xor(is_a, is_helped(s)))

    def mine(s):
        return jnp.where(is_owner(s), t, across_t)

    def theirs(s):
        return jnp.where(is_owner(s), across_t, t)

    def peer_of(d):
        return lax.rem(t + d, n_width)

    def y_of(d):
        return lax.rem(y + d, n_y)

    def at_y(row):
        return {"tensor": x * n_y + row}

    loads = [
        pltpu.make_async_copy(acts_ref.at[0], xbuf.at[dp], load_sem.at[0]),
        pltpu.make_async_copy(gate_ref.at[0], wg, load_sem.at[1]),
        pltpu.make_async_copy(up_ref.at[0], wu, load_sem.at[2]),
    ]
    for load in loads:
        load.start()

    barrier = pltpu.get_barrier_semaphore()
    greeted = [mate, other] + [{"tensor": peer_of(d)} for d in range(1, n_width)]
    for d in range(1, max(reach, 2) + 1):
        greeted += [{"dp": wrap(dp + 2 * d, n_data)}, {"dp": wrap(dp - 2 * d, n_data)}]
    for device in greeted:
        pl.semaphore_signal(barrier, inc=1, device_id=device, device_id_type=MESH)
    pl.semaphore_wait(barrier, len(greeted))

    sides = ((-2, 0, up_s, up_r, 0), (2, 1, dn_s, dn_r, 1))
    acts_ring = (xbuf, tuple((k, pl.ds(k * TILE, TILE)) for k in range(rows // TILE)))
    spread = rows // TILE

    def away(step, d):
        return {"dp": wrap(dp - step * d, n_data)}

    def ring_start(ring):
        buf, pieces = ring
        for d in (2, 1):
            for k, part in pieces:
                own = buf.at[dp, part]
                for step, last_core, ss, rs, _odd in sides:
                    @pl.when((d < half) | (core == last_core))
                    def _():
                        remote(own, own, ss.at[k], rs.at[k, d], away(step, d)).start()
        for k, part in pieces:
            own = buf.at[dp, part]
            remote(own, own, pt_s.at[k], pt_r.at[k, 0], mate).start()

    def ring_mate_own(ring):
        buf, pieces = ring
        for k, part in pieces:
            theirs = buf.at[mate_dp, part]
            remote(theirs, theirs, pt_s.at[k], pt_r.at[k, 0], mate).wait_recv()

    def ring_wave(ring, w):
        buf, pieces = ring
        far = 2 * w
        for d in (far, far - 1):
            for k, part in pieces:
                for step, last_core, ss, rs, odd in sides:
                    @pl.when((d < half) | (core == last_core))
                    def _():
                        ref = buf.at[wrap(dp + step * d, n_data), part]
                        remote(ref, ref, ss.at[k], rs.at[k, d], mate).wait_recv()
                        if d is far:
                            @pl.when((far + 2 < half) | ((far + 2 == half) & (core == last_core)))
                            def _():
                                remote(
                                    ref, ref, ss.at[k], rs.at[k, far + 2], away(step, 2)
                                ).start()

                            @pl.when(far < half)
                            def _():
                                remote(
                                    ref, ref, ss.at[k], rs.at[k, far + 1], away(step, 1)
                                ).start()

                        slot = 2 * d + odd
                        remote(ref, ref, pt_s.at[k], pt_r.at[k, slot], mate).start()

    def ring_mate(ring, s):
        buf, pieces = ring
        for k, part in pieces:
            for step, last_core, _ss, _rs, odd in sides:
                @pl.when((s < half) | (core != last_core))
                def _():
                    ref = buf.at[wrap(mate_dp + step * s, n_data), part]
                    slot = 2 * s + odd
                    remote(ref, ref, pt_s.at[k], pt_r.at[k, slot], mate).wait_recv()

    def ring_drain(buf, pieces):
        for k, part in pieces:
            everything = buf.at[pl.ds(0, n_chip), part]
            remote(everything, everything, pt_s.at[k], pt_r.at[k, 0], mate).wait_send()
            for _step, last_core, ss, rs, _odd in sides:
                for some, count in ((core == last_core, half), (core != last_core, half - 1)):
                    @pl.when(some)
                    def _():
                        ref = buf.at[pl.ds(0, count), part]
                        remote(ref, ref, ss.at[k], rs.at[k, 1], mate).wait_send()

    def panel_start():
        own = panel.at[dp]
        for d in range(reach, 0, -1):
            for step, _last, ss, rs, _odd in sides:
                target = {"dp": wrap(dp - step * d, n_data)}
                remote(own, own, ss.at[spread], rs.at[spread, d], target).start()
        remote(own, own, pt_s.at[spread], pt_r.at[spread, 0], mate).start()

    def panel_take(d, side):
        step, _last, ss, rs, odd = side
        ref = panel.at[wrap(dp + step * d, n_data)]
        remote(ref, ref, ss.at[spread], rs.at[spread, d], mate).wait_recv()
        return ref, remote(
            ref, ref, pt_s.at[spread], pt_r.at[spread, 2 * d + odd], mate
        )

    def panel_take_own():
        own = panel.at[dp]
        remote(own, own, cz_s.at[0], cz_r.at[0], other).wait_recv()

    def panel_forward():
        for side in sides:
            step, last_core, ss, rs, _odd = side
            ref, to_mate = panel_take(reach, side)

            def pass_to(d):
                target = {"dp": wrap(dp - step * d, n_data)}
                return remote(ref, ref, ss.at[spread], rs.at[spread, reach + d], target)

            @pl.when(core == last_core)
            def _():
                pass_to(reach).start()

            for d in range(reach - 1, 0, -1):
                pass_to(d).start()
            to_mate.start()

    def panel_collect():
        for d in range(1, half + 1):
            if d == reach:
                continue
            for side in sides:
                if d < half:
                    panel_take(d, side)[1].start()
                else:
                    @pl.when(core == side[1])
                    def _():
                        panel_take(d, side)[1].start()

    def panel_mate():
        theirs = panel.at[mate_dp]
        remote(theirs, theirs, pt_s.at[spread], pt_r.at[spread, 0], mate).wait_recv()

        def body(d, carry):
            for step, last_core, _ss, _rs, odd in sides:
                @pl.when((d < half) | (core != last_core))
                def _():
                    ref = panel.at[wrap(mate_dp + step * d, n_data)]
                    slot = 2 * d + odd
                    remote(
                        ref, ref, pt_s.at[spread], pt_r.at[spread, slot], mate
                    ).wait_recv()
            return carry

        lax.fori_loop(1, half + 1, body, 0)

    def tile_of(s, who):
        low, high = wrap(chip - s, n_chip), lax.rem(chip + lax.rem(s, half), n_chip)
        return jnp.where(who < n_y, low, high) * n_y + lax.rem(who, n_y)

    def own_copies(s):
        ref = hid_b.at[tile_of(s, mine(s))]
        copies = [remote(ref, ref, gx_s.at[s - 1], gx_r.at[s - 1], across)]
        for d in range(1, n_y):
            row = y_of(d)
            copies.append(remote(ref, ref, g_s.at[s - 1], g_r.at[s - 1], at_y(row)))
        return copies

    def passed_copies(s):
        ref = hid_b.at[tile_of(s, theirs(s))]
        return [
            remote(ref, ref, g_s.at[s - 1], g_r.at[s - 1], at_y(y_of(d)))
            for d in range(1, n_y)
        ]

    def direct_copies(s):
        ref = hid_b.at[tile_of(s, mine(s))]
        return [
            remote(
                ref, ref, g_s.at[s - 1], g_r.at[s - 1],
                {"tensor": (1 - x) * n_y + y_of(d)},
            )
            for d in range(1, n_y)
        ]

    def cross_copy(s, who):
        ref = hid_b.at[tile_of(s, who)]
        return remote(ref, ref, xc_s.at[s - 1], xc_r.at[s - 1], other)

    def pass_on(s):
        ref = hid_b.at[tile_of(s, theirs(s))]
        remote(ref, ref, gx_s.at[s - 1], gx_r.at[s - 1], across).wait_recv()
        for copy in passed_copies(s):
            copy.start()

    def x_copy(s):
        return remote(
            part_b.at[s - 1, pl.ds((1 - x) * n_y, n_y)], got_x.at[s - 1],
            rx_s.at[s - 1], rx_r.at[s - 1], across,
        )

    def raw_copy(s):
        ref = part_b.at[s - 1]
        return remote(ref, ref, px_s.at[s - 1], px_r.at[s - 1], other)

    def full_copy(s, peer):
        k = s // 2 - 1
        return remote(
            part_b.at[s - 1, peer], got_d.at[k, t], rd_s.at[k], rd_r.at[k], {"tensor": peer}
        )

    def full_total(s):
        k = s // 2 - 1
        total = part_b[s - 1, t].astype(F32)
        seven = got_d.at[k, pl.ds(0, n_width - 1)]
        remote(seven, seven, rd_s.at[k], rd_r.at[k], across).wait_recv()
        for d in range(1, n_width):
            src = peer_of(d)
            total = total + got_d[k, src].astype(F32)
        finish(s, total)

    def start_x(s):
        x_copy(s).start()

    def raw(s):
        raw_copy(s).wait_recv()
        x_copy(s).start()

    def y_copy(s, row):
        return remote(
            sum_b.at[s - 1, row], got_y.at[s - 1, y], ry_s.at[s - 1], ry_r.at[s - 1], at_y(row)
        )

    def b_product(s):
        low, high = wrap(chip - s, n_chip), lax.rem(chip + lax.rem(s, half), n_chip)
        left = jnp.concatenate(
            [xbuf[2 * low], xbuf[2 * low + 1], xbuf[2 * high], xbuf[2 * high + 1]], axis=0
        )
        for weight, start in ((wg, 0), (wu, units)):
            part = jnp.dot(left, weight[...], preferred_element_type=F32).astype(BF16)
            part_b[s - 1, :, :, start:start + units] = part.reshape(n_width, TILE, units)
        @pl.when(is_helped(s))
        def _():
            raw_copy(s).start()

        @pl.when(is_full(s))
        def _():
            for d in range(1, n_width):
                full_copy(s, peer_of(d)).start()

        @pl.when(jnp.logical_not(is_helped(s) | is_full(s)) & (s < first_late))
        def _():
            start_x(s)

    def b_pair(s):
        x_copy(s).wait_recv()
        for d in range(1, n_y):
            row = y_of(d)
            pair = part_b[s - 1, x * n_y + row].astype(F32) + got_x[s - 1, row].astype(F32)
            sum_b[s - 1, row] = pair.astype(BF16)
            y_copy(s, row).start()

    def b_total(s):
        total = part_b[s - 1, t].astype(F32) + got_x[s - 1, y].astype(F32)
        three = got_y.at[s - 1, pl.ds(0, n_y - 1)]
        remote(three, three, ry_s.at[s - 1], ry_r.at[s - 1], across).wait_recv()
        for d in range(1, n_y):
            row = y_of(d)
            total = total + got_y[s - 1, row].astype(F32)
        finish(s, total)

    def finish(s, total):
        hid_b[tile_of(s, t)] = silu_times(total[:, :units], total[:, units:])
        cross_copy(s, t).start()
        share(s)

    def share(s):
        @pl.when(is_a | (s not in returned))
        def _():
            for copy in own_copies(s):
                copy.start()

            @pl.when(is_direct(s))
            def _():
                for copy in direct_copies(s):
                    copy.start()

    def back_copies(s):
        k = returned.index(s)
        copies = []
        for d in range(1, n_width):
            who = lax.rem(mine(s) + d, n_width)
            ref = hid_b.at[tile_of(s, who)]
            copies.append(remote(ref, ref, bk_s.at[k], bk_r.at[k], other))
        return copies

    def wait_x(s):
        ref = hid_b.at[tile_of(s, theirs(s))]
        remote(ref, ref, gx_s.at[s - 1], gx_r.at[s - 1], across).wait_recv()

    def six_tiles(s):
        six = hid_b.at[pl.ds(0, 2 * n_y - 2)]
        return remote(six, six, g_s.at[s - 1], g_r.at[s - 1], across)

    def wait_y(s):
        six_tiles(s).wait_recv()

    def seven_tiles(s):
        k = returned.index(s)
        seven = hid_b.at[pl.ds(0, n_width - 1)]
        return remote(seven, seven, bk_s.at[k], bk_r.at[k], other)

    def give_back(s):
        if s not in relayed:
            wait_x(s)
        wait_y(s)
        for copy in back_copies(s):
            copy.start()

    def take(s):
        cross_copy(s, mine(s)).wait_recv()
        share(s)

    def a_select():
        found = table_ref[pl.ds(dp // 8, 2 * n_width, stride=n_data // 8), :]
        found = jnp.broadcast_to(found[:, None, :], (2 * n_width, PICK, 128))
        found = found.reshape(2 * n_width * PICK, 128)
        shape = found.shape
        lane = lax.broadcasted_iota(jnp.int32, shape, 1)
        pick = lax.rem(lax.broadcasted_iota(jnp.int32, shape, 0), PICK)
        wanted = lax.rem(dp, 8) * PICK + pick
        local = jnp.where(lane == wanted, found - dp * units, 0).astype(F32)
        column = jnp.sum(local, axis=1, keepdims=True).astype(jnp.int32)
        unit = lax.broadcasted_iota(jnp.int32, (shape[0], units), 1)
        chosen = jnp.where(unit == column, 1.0, 0.0).astype(BF16)
        for i, weight in enumerate((wg, wu)):
            sel_w[i] = lax.dot_general(
                chosen, weight[...], (((1,), (1,)), ((), ())), preferred_element_type=F32
            ).astype(BF16)

    def a_copy(pair, peer):
        return remote(
            part_a.at[pair, :, peer], got_a.at[t, pair], ra_s.at[0], ra_r.at[0],
            {"tensor": peer},
        )

    def a_product(pair):
        blocks = 128 // rows
        right = xbuf[pl.ds(pair * blocks, blocks)].reshape(128, width)
        for kind in range(2):
            part = lax.dot_general(
                sel_w[kind], right, (((1,), (1,)), ((), ())), preferred_element_type=F32
            ).astype(BF16)
            for r in range(2 * n_width):
                group = r // n_width
                who = (r + group * n_y) % n_width
                part_a[pair, group, who, kind] = part[r * PICK:(r + 1) * PICK]
        for d in range(1, n_width):
            a_copy(pair, peer_of(d)).start()

    def a_chunk(s):
        here = chip // 2
        k = s // 2
        odd = lax.rem(s, 2) == 1

        @pl.when(odd)
        def _():
            a_product(lax.rem(here + k, n_pair))

        @pl.when(odd & (s > 1))
        def _():
            a_product(wrap(here - k, n_pair))

        @pl.when(s == half)
        def _():
            a_product(lax.rem(here + n_pair // 2, n_pair))

    def a_sum():
        others = got_a.at[pl.ds(0, n_width - 1)]
        remote(others, others, ra_s.at[0], ra_r.at[0], across).wait_recv()
        for group in (1, 0):
            pieces = []
            for pair in range(n_pair):
                gate = part_a[pair, group, t, 0].astype(F32)
                up = part_a[pair, group, t, 1].astype(F32)
                for d in range(1, n_width):
                    gate = gate + got_a[peer_of(d), pair, group, 0].astype(F32)
                    up = up + got_a[peer_of(d), pair, group, 1].astype(F32)
                pieces.append(silu_times(gate, up).astype(F32))
            wide = jnp.concatenate(pieces, axis=1)
            mean = jnp.sum(wide, axis=1, keepdims=True) / tokens
            var = jnp.sum(wide * wide, axis=1, keepdims=True) / tokens - mean * mean
            z = ((wide - mean) * lax.rsqrt(var + EPS)).astype(BF16)
            if group == 1:
                cross_z[...] = z
                remote(cross_z, panel.at[dp], cz_s.at[0], cz_r.at[0], other).start()
            else:
                panel[dp] = z

    loads[0].wait()
    ring_start(acts_ring)
    loads[1].wait()
    loads[2].wait()

    @pl.when(is_a)
    def _():
        a_select()

    ring_mate_own(acts_ring)

    def use(s):
        ring_mate(acts_ring, s)

        @pl.when(is_b)
        def _():
            b_product(s)

        @pl.when(is_a)
        def _():
            a_chunk(s)

    owned = [s for s in range(1, half + 1) if s not in helped]
    if half == 8:
        a_late = [
            (raw, 1), (a_sum,), (panel_start,), (take, 2), (raw, 3), (b_pair, 1), (take, 4),
            (pass_on, 2), (b_total, 1), (pass_on, 4), (b_pair, 3), (give_back, 2), (panel_forward,),
            (take, 5), (pass_on, 1), (b_total, 3), (take, 6), (take, 7), (give_back, 4),
            (pass_on, 5), (panel_collect,), (give_back, 1), (take, 8),
        ]
        b_late = [
            (full_total, 2), (full_total, 4), (start_x, 6), (b_pair, 5), (start_x, 7),
            (panel_take_own,), (panel_start,), (b_total, 5), (b_pair, 6), (start_x, 8),
            (panel_forward,), (b_pair, 7), (b_total, 6), (take, 1), (b_total, 7), (b_pair, 8),
            (pass_on, 5), (pass_on, 6), (pass_on, 7), (b_total, 8), (take, 3), (pass_on, 3),
            (panel_collect,),
        ]
    else:
        a_late = [
            *[(act, s) for s in helped for act in (raw, b_pair, b_total)], (a_sum,), (panel_start,),
            *[(take, s) for s in owned], (panel_forward,), *[(give_back, s) for s in returned],
            (panel_collect,),
        ]
        b_late = [
            *[(full_total, s) for s in owned if s in full],
            *[(act, s) for s in owned if s not in full for act in (b_pair, b_total)],
            (panel_take_own,),
            (panel_start,), *[(take, s) for s in helped], (panel_forward,),
            *[(pass_on, s) for s in range(1, half)], (panel_collect,),
        ]

    def gather_wave(w, carry):
        ring_wave(acts_ring, w)

        @pl.when(w > 1)
        def _():
            use(2 * w - 2)

        use(2 * w - 1)
        return carry

    lax.fori_loop(1, half // 2 + 1, gather_wave, 0)
    use(half)

    for model, acts in ((is_a, a_late), (is_b, b_late)):
        @pl.when(model)
        def _():
            for act, *chunk in acts:
                act(*chunk)

    def last(s, carry):
        @pl.when(is_direct(s) & jnp.logical_not(is_returned(s)))
        def _():
            wait_x(s)

        return carry

    ring_drain(*acts_ring)
    ring_drain(panel, ((spread, pl.ds(0, PICK)),))
    lax.fori_loop(1, half + 1, last, 0)
    panel_mate()

    def arrive(s, carry):
        @pl.when(jnp.logical_not(is_returned(s)))
        def _():
            wait_y(s)

        return carry

    @pl.when(is_b)
    def _():
        for s in returned:
            seven_tiles(s).wait_recv()

    lax.fori_loop(1, half + 1, arrive, 0)

    left = panel[...].reshape(n_data * PICK, tokens)
    scale = 1.0 / math.sqrt(tokens)
    start = 0
    while start < units:
        size = min(256, units - start)
        wide = hid_b[:, :, start:start + size].reshape(tokens, size).astype(F32)
        mean = jnp.sum(wide, axis=0, keepdims=True) / tokens
        var = jnp.sum(wide * wide, axis=0, keepdims=True) / tokens - mean * mean
        z = ((wide - mean) * lax.rsqrt(var + EPS)).astype(BF16)
        score = jnp.dot(left, z, preferred_element_type=F32) * scale
        out_ref[:, start:start + size] = score.astype(BF16)
        start += size

    def sent(s, carry):
        @pl.when(is_a | jnp.logical_not(is_returned(s)))
        def _():
            own_copies(s)[0].wait_send()
            six_tiles(s).wait_send()

        @pl.when(is_owner(s))
        def _():
            cross_copy(s, t).wait_send()

            @pl.when(is_full(s))
            def _():
                k = s // 2 - 1
                seven = part_b.at[s - 1, pl.ds(0, n_width - 1)]
                remote(seven, seven, rd_s.at[k], rd_r.at[k], across).wait_send()

            @pl.when(jnp.logical_not(is_full(s)))
            def _():
                x_copy(s).wait_send()
                three = sum_b.at[s - 1, pl.ds(0, n_y - 1)]
                remote(three, three, ry_s.at[s - 1], ry_r.at[s - 1], across).wait_send()

        @pl.when(is_b & is_helped(s))
        def _():
            raw_copy(s).wait_send()

        return carry

    lax.fori_loop(1, half + 1, sent, 0)

    @pl.when(is_a)
    def _():
        remote(cross_z, panel.at[dp], cz_s.at[0], cz_r.at[0], other).wait_send()
        for s in returned:
            seven_tiles(s).wait_send()

        others = part_a.at[:, :, pl.ds(0, n_width - 1)]
        remote(others, others, ra_s.at[0], ra_r.at[0], across).wait_send()


def body(n_data, n_width, acts, gate_w, up_w, panel_units):
    _, rows, width = acts.shape
    units = gate_w.shape[2]
    tokens = n_data * rows
    steps = n_data // 4
    pairs = n_data // 4
    n_y = n_width // 2
    rings = rows // TILE + 1
    hbm = pl.BlockSpec(memory_space=pltpu.HBM)
    vmem = pl.BlockSpec(memory_space=pltpu.VMEM)
    dma = pltpu.SemaphoreType.DMA
    both = lambda *shape: [dma(shape), dma(shape)]
    return pl.pallas_call(
        functools.partial(kernel, n_data, n_width),
        out_shape=jax.ShapeDtypeStruct((n_data * PICK, units), BF16),
        in_specs=[hbm, hbm, hbm, vmem],
        out_specs=vmem,
        scratch_shapes=[
            pltpu.VMEM((n_data, rows, width), BF16),
            pltpu.VMEM((width, units), BF16),
            pltpu.VMEM((width, units), BF16),
            pltpu.VMEM((steps, n_width, TILE, 2 * units), BF16),
            pltpu.VMEM((steps, n_y, TILE, 2 * units), BF16),
            pltpu.VMEM((steps, n_y, TILE, 2 * units), BF16),
            pltpu.VMEM((steps, n_y, TILE, 2 * units), BF16),
            pltpu.VMEM((2, n_width, TILE, 2 * units), BF16),
            pltpu.VMEM((tokens // TILE, TILE, units), BF16),
            pltpu.VMEM((2, 2 * n_width * PICK, width), BF16),
            pltpu.VMEM((pairs, 2, n_width, 2, PICK, 128), BF16),
            pltpu.VMEM((n_width, pairs, 2, 2, PICK, 128), BF16),
            pltpu.VMEM((PICK, tokens), BF16),
            pltpu.VMEM((n_data, PICK, tokens), BF16),
            dma((3,)),
            dma((rings,)),
            dma((rings, steps + 1)),
            dma((rings,)),
            dma((rings, steps + 1)),
            dma((rings,)),
            dma((rings, 2 * steps + 2)),
            *both(steps),
            *both(3),
            *both(2),
            *both(steps),
            *both(steps),
            *both(steps),
            *both(steps),
            *both(steps),
            *both(1),
            *both(1),
        ],
        compiler_params=pltpu.CompilerParams(
            collective_id=0, has_side_effects=True, vmem_limit_bytes=62914560
        ),
    )(acts, gate_w, up_w, panel_units.reshape(-1, 128))


def solution(mesh):
    in_specs = (P("mp", "dp", "tensor"), P("mp", "tensor", "dp"), P("mp", "tensor", "dp"), P())
    out_specs = P(("mp", "tensor"), "dp")
    step = functools.partial(body, mesh.shape["dp"], mesh.shape["tensor"])
    return jax.shard_map(step, mesh=mesh, in_specs=in_specs, out_specs=out_specs, check_vma=False)
```

```python
import functools
import math

import jax
import jax.numpy as jnp
from jax import lax
from jax.experimental import pallas as pl
from jax.experimental.pallas import tpu as pltpu
from jax.sharding import PartitionSpec as P

MESH = pl.DeviceIdType.MESH
F32 = jnp.float32
BF16 = jnp.bfloat16
EPS = 1e-05
TILE = 16
PICK = 16


def wrap(value, n):
    return lax.rem(value + n, n)


def remote(src, dst, send_sem, recv_sem, device):
    return pltpu.make_async_remote_copy(
        src_ref=src,
        dst_ref=dst,
        send_sem=send_sem,
        recv_sem=recv_sem,
        device_id=device,
        device_id_type=MESH,
    )


def silu_times(gate, up):
    return (gate / (1.0 + jnp.exp(-gate)) * up).astype(BF16)


def kernel(
    n_data, n_width, acts_ref, gate_ref, up_ref, table_ref, out_ref,
    xbuf, wg, wu, part_b, got_x, sum_b, got_y, got_d, hid_b, sel_w, part_a, got_a, cross_z, panel,
    load_sem, up_s, up_r, dn_s, dn_r, pt_s, pt_r, px_s, px_r, bk_s, bk_r, rd_s, rd_r, rx_s, rx_r, ry_s, ry_r,
    gx_r, g_s, g_r, xc_s, xc_r, ra_s, ra_r, cz_s, cz_r,
):
    mp = lax.axis_index("mp")
    dp = lax.axis_index("dp")
    t = lax.axis_index("tensor")
    chip = dp // 2
    core = lax.rem(dp, 2)
    n_chip = n_data // 2
    half = n_chip // 2
    reach = half // 2
    n_pair = n_chip // 2
    n_y = n_width // 2
    x = t // n_y
    y = lax.rem(t, n_y)
    rows = acts_ref.shape[1]
    width = acts_ref.shape[2]
    units = gate_ref.shape[2]
    tokens = n_data * rows
    mate_dp = dp + 1 - 2 * core
    mate = {"dp": mate_dp}
    across_t = lax.rem(t + n_y, n_width)
    across = {"tensor": across_t}
    other = {"mp": 1 - mp, "tensor": across_t}
    is_a = mp == 0
    is_b = mp == 1

    helped = [s for s in (1, 3) if s <= half]

    def is_helped(s):
        return functools.reduce(jnp.logical_or, [s == h for h in helped])

    relayed = (1, 2, 4, 5) if half == 8 else ()
    first_late = 6 if half == 8 else half + 1

    def is_direct(s):
        passed = functools.reduce(jnp.logical_or, [s == r for r in relayed], s < 0)
        return jnp.where(is_a, jnp.logical_not(passed), s == half)

    full = [s for s in (2, 4) if s <= half]

    def is_full(s):
        return functools.reduce(jnp.logical_or, [s == f for f in full])

    returned = [s for s in ((1, 2, 4) if half == 8 else (2,)) if s <= half]

    def is_returned(s):
        return functools.reduce(jnp.logical_or, [s == r for r in returned])

    def is_owner(s):
        return jnp.logical_not(jnp.logical_xor(is_a, is_helped(s)))

    def mine(s):
        return jnp.where(is_owner(s), t, across_t)

    def theirs(s):
        return jnp.where(is_owner(s), across_t, t)

    def peer_of(d):
        return lax.rem(t + d, n_width)

    def y_of(d):
        return lax.rem(y + d, n_y)

    def at_y(row):
        return {"tensor": x * n_y + row}

    loads = [
        pltpu.make_async_copy(acts_ref.at[0], xbuf.at[dp], load_sem.at[0]),
        pltpu.make_async_copy(gate_ref.at[0], wg, load_sem.at[1]),
        pltpu.make_async_copy(up_ref.at[0], wu, load_sem.at[2]),
    ]
    for load in loads:
        load.start()

    barrier = pltpu.get_barrier_semaphore()
    greeted = [mate, other] + [{"tensor": peer_of(d)} for d in range(1, n_width)]
    for d in range(1, max(reach, 2) + 1):
        greeted += [{"dp": wrap(dp + 2 * d, n_data)}, {"dp": wrap(dp - 2 * d, n_data)}]
    for device in greeted:
        pl.semaphore_signal(barrier, inc=1, device_id=device, device_id_type=MESH)
    pl.semaphore_wait(barrier, len(greeted))

    sides = ((-2, 0, up_s, up_r, 0), (2, 1, dn_s, dn_r, 1))
    acts_ring = (xbuf, tuple((k, pl.ds(k * TILE, TILE)) for k in range(rows // TILE)))
    spread = rows // TILE

    def away(step, d):
        return {"dp": wrap(dp - step * d, n_data)}

    def ring_start(ring):
        buf, pieces = ring
        for d in (2, 1):
            for k, part in pieces:
                own = buf.at[dp, part]
                for step, last_core, ss, rs, _odd in sides:
                    @pl.when((d < half) | (core == last_core))
                    def _():
                        remote(own, own, ss.at[k], rs.at[k, d], away(step, d)).start()
        for k, part in pieces:
            own = buf.at[dp, part]
            remote(own, own, pt_s.at[k], pt_r.at[k, 0], mate).start()

    def ring_mate_own(ring):
        buf, pieces = ring
        for k, part in pieces:
            theirs = buf.at[mate_dp, part]
            remote(theirs, theirs, pt_s.at[k], pt_r.at[k, 0], mate).wait_recv()

    def ring_wave(ring, w):
        buf, pieces = ring
        far = 2 * w
        for d in (far, far - 1):
            for k, part in pieces:
                for step, last_core, ss, rs, odd in sides:
                    @pl.when((d < half) | (core == last_core))
                    def _():
                        ref = buf.at[wrap(dp + step * d, n_data), part]
                        remote(ref, ref, ss.at[k], rs.at[k, d], mate).wait_recv()
                        if d is far:
                            @pl.when((far + 2 < half) | ((far + 2 == half) & (core == last_core)))
                            def _():
                                remote(
                                    ref, ref, ss.at[k], rs.at[k, far + 2], away(step, 2)
                                ).start()

                            @pl.when(far < half)
                            def _():
                                remote(
                                    ref, ref, ss.at[k], rs.at[k, far + 1], away(step, 1)
                                ).start()

                        slot = 2 * d + odd
                        remote(ref, ref, pt_s.at[k], pt_r.at[k, slot], mate).start()

    def ring_mate(ring, s):
        buf, pieces = ring
        for k, part in pieces:
            for step, last_core, _ss, _rs, odd in sides:
                @pl.when((s < half) | (core != last_core))
                def _():
                    ref = buf.at[wrap(mate_dp + step * s, n_data), part]
                    slot = 2 * s + odd
                    remote(ref, ref, pt_s.at[k], pt_r.at[k, slot], mate).wait_recv()

    def ring_drain(buf, pieces):
        for k, part in pieces:
            everything = buf.at[pl.ds(0, n_chip), part]
            remote(everything, everything, pt_s.at[k], pt_r.at[k, 0], mate).wait_send()
            for _step, last_core, ss, rs, _odd in sides:
                for some, count in ((core == last_core, half), (core != last_core, half - 1)):
                    @pl.when(some)
                    def _():
                        ref = buf.at[pl.ds(0, count), part]
                        remote(ref, ref, ss.at[k], rs.at[k, 1], mate).wait_send()

    def panel_start():
        own = panel.at[dp]
        for d in range(reach, 0, -1):
            for step, _last, ss, rs, _odd in sides:
                target = {"dp": wrap(dp - step * d, n_data)}
                remote(own, own, ss.at[spread], rs.at[spread, d], target).start()
        remote(own, own, pt_s.at[spread], pt_r.at[spread, 0], mate).start()

    def panel_take(d, side):
        step, _last, ss, rs, odd = side
        ref = panel.at[wrap(dp + step * d, n_data)]
        remote(ref, ref, ss.at[spread], rs.at[spread, d], mate).wait_recv()
        return ref, remote(
            ref, ref, pt_s.at[spread], pt_r.at[spread, 2 * d + odd], mate
        )

    def panel_take_own():
        own = panel.at[dp]
        remote(own, own, cz_s.at[0], cz_r.at[0], other).wait_recv()

    def panel_forward():
        for side in sides:
            step, last_core, ss, rs, _odd = side
            ref, to_mate = panel_take(reach, side)

            def pass_to(d):
                target = {"dp": wrap(dp - step * d, n_data)}
                return remote(ref, ref, ss.at[spread], rs.at[spread, reach + d], target)

            @pl.when(core == last_core)
            def _():
                pass_to(reach).start()

            for d in range(reach - 1, 0, -1):
                pass_to(d).start()
            to_mate.start()

    def panel_collect():
        for d in range(1, half + 1):
            if d == reach:
                continue
            for side in sides:
                if d < half:
                    panel_take(d, side)[1].start()
                else:
                    @pl.when(core == side[1])
                    def _():
                        panel_take(d, side)[1].start()

    def panel_mate():
        theirs = panel.at[mate_dp]
        remote(theirs, theirs, pt_s.at[spread], pt_r.at[spread, 0], mate).wait_recv()

        def body(d, carry):
            for step, last_core, _ss, _rs, odd in sides:
                @pl.when((d < half) | (core != last_core))
                def _():
                    ref = panel.at[wrap(mate_dp + step * d, n_data)]
                    slot = 2 * d + odd
                    remote(
                        ref, ref, pt_s.at[spread], pt_r.at[spread, slot], mate
                    ).wait_recv()
            return carry

        lax.fori_loop(1, half + 1, body, 0)

    def tile_of(s, who):
        low, high = wrap(chip - s, n_chip), lax.rem(chip + lax.rem(s, half), n_chip)
        return jnp.where(who < n_y, low, high) * n_y + lax.rem(who, n_y)

    def own_copies(s):
        ref = hid_b.at[tile_of(s, mine(s))]
        copies = [remote(ref, ref, g_s.at[s - 1], gx_r.at[s - 1], across)]
        for d in range(1, n_y):
            row = y_of(d)
            copies.append(remote(ref, ref, g_s.at[s - 1], g_r.at[s - 1], at_y(row)))
        return copies

    def passed_copies(s):
        ref = hid_b.at[tile_of(s, theirs(s))]
        return [
            remote(ref, ref, g_s.at[s - 1], g_r.at[s - 1], at_y(y_of(d)))
            for d in range(1, n_y)
        ]

    def direct_copies(s):
        ref = hid_b.at[tile_of(s, mine(s))]
        return [
            remote(
                ref, ref, g_s.at[s - 1], g_r.at[s - 1],
                {"tensor": (1 - x) * n_y + y_of(d)},
            )
            for d in range(1, n_y)
        ]

    def cross_copy(s, who):
        ref = hid_b.at[tile_of(s, who)]
        return remote(ref, ref, xc_s.at[s - 1], xc_r.at[s - 1], other)

    def pass_on(s):
        ref = hid_b.at[tile_of(s, theirs(s))]
        remote(ref, ref, g_s.at[s - 1], gx_r.at[s - 1], across).wait_recv()
        for copy in passed_copies(s):
            copy.start()

    def x_copy(s):
        return remote(
            part_b.at[s - 1, pl.ds((1 - x) * n_y, n_y)], got_x.at[s - 1],
            rx_s.at[s - 1], rx_r.at[s - 1], across,
        )

    def raw_copy(s):
        ref = part_b.at[s - 1]
        return remote(ref, ref, px_s.at[s // 2], px_r.at[s // 2], other)

    def full_copy(s, peer):
        k = s // 2 - 1
        return remote(
            part_b.at[s - 1, peer], got_d.at[k, t], rd_s.at[k], rd_r.at[k], {"tensor": peer}
        )

    def full_total(s):
        k = s // 2 - 1
        total = part_b[s - 1, t].astype(F32)
        seven = got_d.at[k, pl.ds(0, n_width - 1)]
        remote(seven, seven, rd_s.at[k], rd_r.at[k], across).wait_recv()
        for d in range(1, n_width):
            src = peer_of(d)
            total = total + got_d[k, src].astype(F32)
        finish(s, total)

    def start_x(s):
        x_copy(s).start()

    def raw(s):
        raw_copy(s).wait_recv()
        x_copy(s).start()

    def y_copy(s, row):
        return remote(
            sum_b.at[s - 1, row], got_y.at[s - 1, y], ry_s.at[s - 1], ry_r.at[s - 1], at_y(row)
        )

    def b_product(s):
        low, high = wrap(chip - s, n_chip), lax.rem(chip + lax.rem(s, half), n_chip)
        left = jnp.concatenate(
            [xbuf[2 * low], xbuf[2 * low + 1], xbuf[2 * high], xbuf[2 * high + 1]], axis=0
        )
        for weight, start in ((wg, 0), (wu, units)):
            part = jnp.dot(left, weight[...], preferred_element_type=F32).astype(BF16)
            part_b[s - 1, :, :, start:start + units] = part.reshape(n_width, TILE, units)
        @pl.when(is_helped(s))
        def _():
            raw_copy(s).start()

        @pl.when(is_full(s))
        def _():
            for d in range(1, n_width):
                full_copy(s, peer_of(d)).start()

        @pl.when(jnp.logical_not(is_helped(s) | is_full(s)) & (s < first_late))
        def _():
            start_x(s)

    def b_pair(s):
        x_copy(s).wait_recv()
        for d in range(1, n_y):
            row = y_of(d)
            pair = part_b[s - 1, x * n_y + row].astype(F32) + got_x[s - 1, row].astype(F32)
            sum_b[s - 1, row] = pair.astype(BF16)
            y_copy(s, row).start()

    def b_total(s):
        total = part_b[s - 1, t].astype(F32) + got_x[s - 1, y].astype(F32)
        three = got_y.at[s - 1, pl.ds(0, n_y - 1)]
        remote(three, three, ry_s.at[s - 1], ry_r.at[s - 1], across).wait_recv()
        for d in range(1, n_y):
            row = y_of(d)
            total = total + got_y[s - 1, row].astype(F32)
        finish(s, total)

    def finish(s, total):
        hid_b[tile_of(s, t)] = silu_times(total[:, :units], total[:, units:])
        cross_copy(s, t).start()
        share(s)

    def share(s):
        @pl.when(is_a | (s not in returned))
        def _():
            for copy in own_copies(s):
                copy.start()

            @pl.when(is_direct(s))
            def _():
                for copy in direct_copies(s):
                    copy.start()

    def back_copies(s):
        k = returned.index(s)
        copies = []
        for d in range(1, n_width):
            who = lax.rem(mine(s) + d, n_width)
            ref = hid_b.at[tile_of(s, who)]
            copies.append(remote(ref, ref, bk_s.at[k], bk_r.at[k], other))
        return copies

    def wait_x(s):
        ref = hid_b.at[tile_of(s, theirs(s))]
        remote(ref, ref, g_s.at[s - 1], gx_r.at[s - 1], across).wait_recv()

    def six_tiles(s):
        six = hid_b.at[pl.ds(0, 2 * n_y - 2)]
        return remote(six, six, g_s.at[s - 1], g_r.at[s - 1], across)

    def wait_y(s):
        six_tiles(s).wait_recv()

    def seven_tiles(s):
        k = returned.index(s)
        seven = hid_b.at[pl.ds(0, n_width - 1)]
        return remote(seven, seven, bk_s.at[k], bk_r.at[k], other)

    def give_back(s):
        if s not in relayed:
            wait_x(s)
        wait_y(s)
        for copy in back_copies(s):
            copy.start()

    def take(s):
        cross_copy(s, mine(s)).wait_recv()
        share(s)

    def a_select():
        found = table_ref[pl.ds(dp // 8, 2 * n_width, stride=n_data // 8), :]
        found = jnp.broadcast_to(found[:, None, :], (2 * n_width, PICK, 128))
        found = found.reshape(2 * n_width * PICK, 128)
        shape = found.shape
        lane = lax.broadcasted_iota(jnp.int32, shape, 1)
        pick = lax.rem(lax.broadcasted_iota(jnp.int32, shape, 0), PICK)
        wanted = lax.rem(dp, 8) * PICK + pick
        local = jnp.where(lane == wanted, found - dp * units, 0).astype(F32)
        column = jnp.sum(local, axis=1, keepdims=True).astype(jnp.int32)
        unit = lax.broadcasted_iota(jnp.int32, (shape[0], units), 1)
        chosen = jnp.where(unit == column, 1.0, 0.0).astype(BF16)
        for i, weight in enumerate((wg, wu)):
            sel_w[i] = lax.dot_general(
                chosen, weight[...], (((1,), (1,)), ((), ())), preferred_element_type=F32
            ).astype(BF16)

    def a_copy(pair, peer):
        return remote(
            part_a.at[pair, :, peer], got_a.at[t, pair], ra_s.at[0], ra_r.at[0],
            {"tensor": peer},
        )

    def a_product(pair):
        blocks = 128 // rows
        right = xbuf[pl.ds(pair * blocks, blocks)].reshape(128, width)
        for kind in range(2):
            part = lax.dot_general(
                sel_w[kind], right, (((1,), (1,)), ((), ())), preferred_element_type=F32
            ).astype(BF16)
            for r in range(2 * n_width):
                group = r // n_width
                who = (r + group * n_y) % n_width
                part_a[pair, group, who, kind] = part[r * PICK:(r + 1) * PICK]
        for d in range(1, n_width):
            a_copy(pair, peer_of(d)).start()

    def a_chunk(s):
        here = chip // 2
        k = s // 2
        odd = lax.rem(s, 2) == 1

        @pl.when(odd)
        def _():
            a_product(lax.rem(here + k, n_pair))

        @pl.when(odd & (s > 1))
        def _():
            a_product(wrap(here - k, n_pair))

        @pl.when(s == half)
        def _():
            a_product(lax.rem(here + n_pair // 2, n_pair))

    def a_sum():
        others = got_a.at[pl.ds(0, n_width - 1)]
        remote(others, others, ra_s.at[0], ra_r.at[0], across).wait_recv()
        for group in (1, 0):
            pieces = []
            for pair in range(n_pair):
                gate = part_a[pair, group, t, 0].astype(F32)
                up = part_a[pair, group, t, 1].astype(F32)
                for d in range(1, n_width):
                    gate = gate + got_a[peer_of(d), pair, group, 0].astype(F32)
                    up = up + got_a[peer_of(d), pair, group, 1].astype(F32)
                pieces.append(silu_times(gate, up).astype(F32))
            wide = jnp.concatenate(pieces, axis=1)
            mean = jnp.sum(wide, axis=1, keepdims=True) / tokens
            var = jnp.sum(wide * wide, axis=1, keepdims=True) / tokens - mean * mean
            z = ((wide - mean) * lax.rsqrt(var + EPS)).astype(BF16)
            if group == 1:
                cross_z[...] = z
                remote(cross_z, panel.at[dp], cz_s.at[0], cz_r.at[0], other).start()
            else:
                panel[dp] = z

    loads[0].wait()
    ring_start(acts_ring)
    loads[1].wait()
    loads[2].wait()

    @pl.when(is_a)
    def _():
        a_select()

    ring_mate_own(acts_ring)

    def use(s):
        ring_mate(acts_ring, s)

        @pl.when(is_b)
        def _():
            b_product(s)

        @pl.when(is_a)
        def _():
            a_chunk(s)

    owned = [s for s in range(1, half + 1) if s not in helped]
    if half == 8:
        a_late = [
            (raw, 1), (a_sum,), (panel_start,), (take, 2), (raw, 3), (b_pair, 1), (take, 4),
            (pass_on, 2), (b_total, 1), (pass_on, 4), (b_pair, 3), (give_back, 2), (panel_forward,),
            (take, 5), (pass_on, 1), (b_total, 3), (take, 6), (take, 7), (give_back, 4),
            (pass_on, 5), (panel_collect,), (give_back, 1), (take, 8),
        ]
        b_late = [
            (full_total, 2), (full_total, 4), (start_x, 6), (b_pair, 5), (start_x, 7),
            (panel_take_own,), (panel_start,), (b_total, 5), (b_pair, 6), (start_x, 8),
            (panel_forward,), (b_pair, 7), (b_total, 6), (take, 1), (b_total, 7), (b_pair, 8),
            (pass_on, 5), (pass_on, 6), (pass_on, 7), (b_total, 8), (take, 3), (pass_on, 3),
            (panel_collect,),
        ]
    else:
        a_late = [
            *[(act, s) for s in helped for act in (raw, b_pair, b_total)], (a_sum,), (panel_start,),
            *[(take, s) for s in owned], (panel_forward,), *[(give_back, s) for s in returned],
            (panel_collect,),
        ]
        b_late = [
            *[(full_total, s) for s in owned if s in full],
            *[(act, s) for s in owned if s not in full for act in (b_pair, b_total)],
            (panel_take_own,),
            (panel_start,), *[(take, s) for s in helped], (panel_forward,),
            *[(pass_on, s) for s in range(1, half)], (panel_collect,),
        ]

    def gather_wave(w, carry):
        ring_wave(acts_ring, w)

        @pl.when(w > 1)
        def _():
            use(2 * w - 2)

        use(2 * w - 1)
        return carry

    lax.fori_loop(1, half // 2 + 1, gather_wave, 0)
    use(half)

    for model, acts in ((is_a, a_late), (is_b, b_late)):
        @pl.when(model)
        def _():
            for act, *chunk in acts:
                act(*chunk)

    def last(s, carry):
        @pl.when(is_direct(s) & jnp.logical_not(is_returned(s)))
        def _():
            wait_x(s)

        return carry

    ring_drain(*acts_ring)
    ring_drain(panel, ((spread, pl.ds(0, PICK)),))
    lax.fori_loop(1, half + 1, last, 0)
    panel_mate()

    def arrive(s, carry):
        @pl.when(jnp.logical_not(is_returned(s)))
        def _():
            wait_y(s)

        return carry

    @pl.when(is_b)
    def _():
        for s in returned:
            seven_tiles(s).wait_recv()

    lax.fori_loop(1, half + 1, arrive, 0)

    left = panel[...].reshape(n_data * PICK, tokens)
    scale = 1.0 / math.sqrt(tokens)
    start = 0
    while start < units:
        size = min(256, units - start)
        wide = hid_b[:, :, start:start + size].reshape(tokens, size).astype(F32)
        mean = jnp.sum(wide, axis=0, keepdims=True) / tokens
        var = jnp.sum(wide * wide, axis=0, keepdims=True) / tokens - mean * mean
        z = ((wide - mean) * lax.rsqrt(var + EPS)).astype(BF16)
        score = jnp.dot(left, z, preferred_element_type=F32) * scale
        out_ref[:, start:start + size] = score.astype(BF16)
        start += size

    def sent(s, carry):
        @pl.when(is_a | jnp.logical_not(is_returned(s)))
        def _():
            sent_tiles = hid_b.at[pl.ds(0, n_width - 1)]
            remote(sent_tiles, sent_tiles, g_s.at[s - 1], g_r.at[s - 1], across).wait_send()

        @pl.when(is_owner(s))
        def _():
            cross_copy(s, t).wait_send()

            @pl.when(is_full(s))
            def _():
                k = s // 2 - 1
                seven = part_b.at[s - 1, pl.ds(0, n_width - 1)]
                remote(seven, seven, rd_s.at[k], rd_r.at[k], across).wait_send()

            @pl.when(jnp.logical_not(is_full(s)))
            def _():
                x_copy(s).wait_send()
                three = sum_b.at[s - 1, pl.ds(0, n_y - 1)]
                remote(three, three, ry_s.at[s - 1], ry_r.at[s - 1], across).wait_send()

        @pl.when(is_b & is_helped(s))
        def _():
            raw_copy(s).wait_send()

        return carry

    lax.fori_loop(1, half + 1, sent, 0)

    @pl.when(is_a)
    def _():
        remote(cross_z, panel.at[dp], cz_s.at[0], cz_r.at[0], other).wait_send()
        for s in returned:
            seven_tiles(s).wait_send()

        others = part_a.at[:, :, pl.ds(0, n_width - 1)]
        remote(others, others, ra_s.at[0], ra_r.at[0], across).wait_send()


def body(n_data, n_width, acts, gate_w, up_w, panel_units):
    _, rows, width = acts.shape
    units = gate_w.shape[2]
    tokens = n_data * rows
    steps = n_data // 4
    pairs = n_data // 4
    n_y = n_width // 2
    rings = rows // TILE + 1
    hbm = pl.BlockSpec(memory_space=pltpu.HBM)
    vmem = pl.BlockSpec(memory_space=pltpu.VMEM)
    dma = pltpu.SemaphoreType.DMA
    both = lambda *shape: [dma(shape), dma(shape)]
    return pl.pallas_call(
        functools.partial(kernel, n_data, n_width),
        out_shape=jax.ShapeDtypeStruct((n_data * PICK, units), BF16),
        in_specs=[hbm, hbm, hbm, vmem],
        out_specs=vmem,
        scratch_shapes=[
            pltpu.VMEM((n_data, rows, width), BF16),
            pltpu.VMEM((width, units), BF16),
            pltpu.VMEM((width, units), BF16),
            pltpu.VMEM((steps, n_width, TILE, 2 * units), BF16),
            pltpu.VMEM((steps, n_y, TILE, 2 * units), BF16),
            pltpu.VMEM((steps, n_y, TILE, 2 * units), BF16),
            pltpu.VMEM((steps, n_y, TILE, 2 * units), BF16),
            pltpu.VMEM((2, n_width, TILE, 2 * units), BF16),
            pltpu.VMEM((tokens // TILE, TILE, units), BF16),
            pltpu.VMEM((2, 2 * n_width * PICK, width), BF16),
            pltpu.VMEM((pairs, 2, n_width, 2, PICK, 128), BF16),
            pltpu.VMEM((n_width, pairs, 2, 2, PICK, 128), BF16),
            pltpu.VMEM((PICK, tokens), BF16),
            pltpu.VMEM((n_data, PICK, tokens), BF16),
            dma((3,)),
            dma((rings,)),
            dma((rings, steps + 1)),
            dma((rings,)),
            dma((rings, steps + 1)),
            dma((rings,)),
            dma((rings, 2 * steps + 2)),
            *both(2),
            *both(3),
            *both(2),
            *both(steps),
            *both(steps),
            dma((steps,)),
            *both(steps),
            *both(steps),
            *both(1),
            *both(1),
        ],
        compiler_params=pltpu.CompilerParams(
            collective_id=0, has_side_effects=True, vmem_limit_bytes=62914560
        ),
    )(acts, gate_w, up_w, panel_units.reshape(-1, 128))


def solution(mesh):
    in_specs = (P("mp", "dp", "tensor"), P("mp", "tensor", "dp"), P("mp", "tensor", "dp"), P())
    out_specs = P(("mp", "tensor"), "dp")
    step = functools.partial(body, mesh.shape["dp"], mesh.shape["tensor"])
    return jax.shard_map(step, mesh=mesh, in_specs=in_specs, out_specs=out_specs, check_vma=False)
```
